32 devices in a mesh: grp: 2 (over core), mr: 8 (over z, y), mc: 2 (over x).
Axes of the slice: x: 2, y: 2, z: 4, core: 2. Of those that a mesh axis runs over, the one named last changes fastest.
Arguments:
- queries: bfloat16 [384, 8192], P(('grp', 'mr'), 'mc'), may hold values from -6 to 6
- new_keys: bfloat16 [384, 1024], P(('grp', 'mr'), 'mc'), may hold values from -6 to 6
- new_values: bfloat16 [384, 1024], P(('grp', 'mr'), 'mc'), may hold values from -6 to 6
- key_cache: bfloat16 [384, 512, 1024], P(('grp', 'mr'), None, 'mc'), may hold values from -6 to 6
- value_cache: bfloat16 [384, 512, 1024], P(('grp', 'mr'), None, 'mc'), may hold values from -6 to 6
- context_len: int32 [384], P(('grp', 'mr')), may hold values from 2 to 512, as said below
- cache_slot: int32 [384], P(('grp', 'mr')), may hold values from 0 to 383, as said below
- residual_in: bfloat16 [384, 8192], P(('grp', 'mr'), 'mc'), may hold values from -31 to 31
- out_weight: bfloat16 [8192, 8192], P(('grp', 'mr'), 'mc'), may hold values from -0.25 to 0.25
- gate_weight: bfloat16 [8192, 28672], P('mc', ('grp', 'mr')), may hold values from -0.0625 to 0.0625
- up_weight: bfloat16 [8192, 28672], P('mc', ('grp', 'mr')), may hold values from -0.0625 to 0.0625
Outputs:
- residual_out: bfloat16 [384, 8192], P(('grp', 'mr'), 'mc')
- activation: bfloat16 [384, 28672], P('mc', ('grp', 'mr'))
The draws below stay inside these ranges and needn't reach their ends.
Inputs may be any that keep to these rules, and one draw needn't show every extreme that they name: Row r's history fills positions 0 to context_len[r] - 1 of its cache row; some row has 512. `cache_slot`: within each aligned block of 24 rows the values are a permutation of that block's own row indices.
All inputs are finite; a program needn't handle non-finite values.
Results may differ from the reference program's by a relative error of at most 0.006.
Values may be sent and summed in bfloat16 or wider, within the bound.
A program may use at most 128 MiB of HBM per device.

```python
import jax
import jax.numpy as jnp
from jax import lax

D = 8192
H = 64
KVH = 8
HD = 128
FF = 28672
CTX = 512
ROWS_DEV = 24
ROWS = 384


def draw_queries(key, part):
    current_key = jax.random.fold_in(key, 17)
    values = jax.random.truncated_normal(current_key, -6.0, 6.0, (ROWS, H * HD), jnp.float32)
    return values.astype(jnp.bfloat16)


def draw_key_cache(key, part):
    current_key = jax.random.fold_in(key, 29)
    values = jax.random.truncated_normal(current_key, -6.0, 6.0, (ROWS, CTX, KVH * HD), jnp.float32)
    return values.astype(jnp.bfloat16)


def draw_residual_in(key, part):
    column = jnp.arange(D, dtype=jnp.float32) / D
    values = jax.random.truncated_normal(key, -6.0, 6.0, (ROWS, D), jnp.float32) * (3.0 ** column)[None, :]
    return values.astype(jnp.bfloat16)


def draw_context_len(key, part):
    length_key, longest_key = jax.random.split(jax.random.fold_in(key, 41))
    values = jax.random.randint(length_key, (ROWS,), 2, CTX + 1)
    longest = jax.random.randint(longest_key, (), 0, ROWS)
    return jnp.where(jnp.arange(ROWS) == longest, CTX, values).astype(jnp.int32)


def shuffle_block(tile_key_rows):
    return jax.random.permutation(tile_key_rows, ROWS_DEV)


def draw_cache_slot(key, part):
    block_count = ROWS // ROWS_DEV
    block_keys = jax.random.split(jax.random.fold_in(key, 53), block_count)
    orders = jax.vmap(shuffle_block)(block_keys)
    offsets = jnp.arange(block_count, dtype=jnp.int32)[:, None] * ROWS_DEV
    return (orders.astype(jnp.int32) + offsets).reshape(ROWS).astype(jnp.int32)


def block_scale(key, dims, cuts, low, largest):
    gain = 1.0
    for dim, blocks in cuts:
        draws = jax.random.uniform(jax.random.fold_in(jax.random.fold_in(key, 6), dim), (blocks,), jnp.float32, low / len(cuts), largest / len(cuts))
        gain = gain * jnp.repeat(jnp.exp(draws), dims[dim] // blocks).reshape((-1,) + (1,) * (len(dims) - 1 - dim))
    return gain


def scatter_about(rng, shape, scale, bound, pieces=(), kind=jnp.bfloat16):
    array = jax.random.normal(rng, shape, jnp.float32) * scale
    if len(pieces) > 0:
        array = block_scale(rng, shape, pieces, -0.22, 0.18) * array
    return jnp.clip(array, min=-bound, max=bound).astype(kind)


def setup_inputs(seed: int = 0) -> dict:
    key_list = jax.random.split(jax.random.key(seed), 12)
    queries = draw_queries(jax.random.fold_in(key_list[11], 71), 0)
    new_keys = scatter_about(key_list[1], (ROWS, KVH * HD), 1.0, 6.0, ((0, 16), (1, 2)))
    new_values = scatter_about(key_list[2], (ROWS, KVH * HD), 1.0, 6.0, ((0, 16), (1, 2)))
    key_cache = draw_key_cache(jax.random.fold_in(key_list[11], 71), 0)
    value_cache = scatter_about(key_list[4], (ROWS, CTX, KVH * HD), 1.0, 6.0, ((0, 16), (2, 2)))
    context_len = draw_context_len(jax.random.fold_in(key_list[11], 71), 0)
    cache_slot = draw_cache_slot(jax.random.fold_in(key_list[11], 71), 0)
    residual_in = draw_residual_in(jax.random.fold_in(key_list[11], 71), 0)
    out_weight = scatter_about(key_list[8], (H * HD, D), (H * 8) ** -0.5, 0.25, ((0, 16), (1, 2)))
    gate_weight = scatter_about(key_list[9], (D, FF), D ** -0.5, 0.0625, ((0, 2), (1, 16)))
    up_weight = scatter_about(key_list[10], (D, FF), D ** -0.5, 0.0625, ((0, 2), (1, 16)))
    return {"queries": queries, "new_keys": new_keys, "new_values": new_values, "key_cache": key_cache, "value_cache": value_cache, "context_len": context_len, "cache_slot": cache_slot, "residual_in": residual_in, "out_weight": out_weight, "gate_weight": gate_weight, "up_weight": up_weight}


norm_epsilon = 1e-05
masked_score = -1e+30

def attend_block(queries, new_keys, new_values, key_rows, value_rows, context_len):
    row_denominator_sum = queries.shape[0]
    kv_heads = key_rows.shape[2] // HD
    groups = queries.shape[1] // key_rows.shape[2]
    attention_logit_scale = HD ** (-0.5)
    query_grouped_four = queries.astype(jnp.float32).reshape(row_denominator_sum, kv_heads, groups, HD)
    key_four = key_rows.astype(jnp.float32).reshape(row_denominator_sum, CTX, kv_heads, HD)
    value_four = value_rows.astype(jnp.float32).reshape(row_denominator_sum, CTX, kv_heads, HD)
    current_key = new_keys.astype(jnp.float32).reshape(row_denominator_sum, kv_heads, HD)
    own_value = new_values.astype(jnp.float32).reshape(row_denominator_sum, kv_heads, HD)
    scores = jnp.einsum('bkgd,bckd->bkgc', query_grouped_four, key_four) * attention_logit_scale
    positions = jnp.arange(CTX, dtype=jnp.int32)
    valid_mask = positions[None, :] < context_len[:, None]
    scores = jnp.where(valid_mask[:, None, None, :], scores, masked_score)
    current_score = jnp.einsum('cnhz,cnz->cnh', query_grouped_four, current_key) * attention_logit_scale
    row_max = jnp.maximum(lax.optimization_barrier(jnp.max(scores, axis=3)), current_score)
    exponent = jnp.exp(scores - row_max[..., None])
    own_exponent = jnp.exp(current_score - row_max)
    denominator = lax.optimization_barrier(jnp.sum(exponent, axis=3)) + own_exponent
    weights = lax.optimization_barrier((exponent / denominator[..., None]).astype(jnp.bfloat16)).astype(jnp.float32)
    own_weight = lax.optimization_barrier((own_exponent / denominator).astype(jnp.bfloat16)).astype(jnp.float32)
    combined = jnp.einsum('bkgc,bckd->bkgd', weights, value_four)
    combined = combined + own_weight[..., None] * own_value[:, :, None, :]
    return combined.reshape(row_denominator_sum, -1).astype(jnp.bfloat16)

def reference(queries, new_keys, new_values, key_cache, value_cache, context_len, cache_slot, residual_in, out_weight, gate_weight, up_weight):
    block_count = ROWS // ROWS_DEV

    def one_block(block_index):
        row_start = (block_index * ROWS_DEV).astype(jnp.int32)
        slot_rows = lax.dynamic_slice_in_dim(cache_slot, row_start, ROWS_DEV)
        key_rows = jnp.take(key_cache, slot_rows, axis=0)
        value_rows = jnp.take(value_cache, slot_rows, axis=0)
        return attend_block(lax.dynamic_slice_in_dim(queries, row_start, ROWS_DEV), lax.dynamic_slice_in_dim(new_keys, row_start, ROWS_DEV), lax.dynamic_slice_in_dim(new_values, row_start, ROWS_DEV), key_rows, value_rows, lax.dynamic_slice_in_dim(context_len, row_start, ROWS_DEV))
    attended = lax.map(one_block, jnp.arange(block_count, dtype=jnp.int32))
    attended = attended.reshape(ROWS, H * HD)
    output_projected = jnp.dot(attended, out_weight, preferred_element_type=jnp.float32)
    residual_out = (residual_in.astype(jnp.float32) + output_projected).astype(jnp.bfloat16)
    widened = lax.optimization_barrier(residual_out).astype(jnp.float32)
    squares = lax.optimization_barrier(jnp.sum(widened * widened, axis=1))
    inverse_rms = lax.rsqrt(squares / D + norm_epsilon)
    gate_value = jnp.dot(residual_out, gate_weight, preferred_element_type=jnp.float32) * inverse_rms[:, None]
    upward = jnp.dot(residual_out, up_weight, preferred_element_type=jnp.float32) * inverse_rms[:, None]
    activation = (jax.nn.silu(gate_value) * upward).astype(jnp.bfloat16)
    return (residual_out, activation)
```

```python
import jax
import jax.numpy as jnp
from jax import lax
from jax.sharding import PartitionSpec as P

D = 8192
HD = 128


norm_epsilon = 1e-05
masked_score = -1e30


def attend_rows(queries, new_keys, new_values, key_rows, value_rows, context_len):
    row_denominator_sum = queries.shape[0]
    context = key_rows.shape[1]
    kv_heads = key_rows.shape[2] // HD
    groups = queries.shape[1] // key_rows.shape[2]
    attention_logit_scale = HD ** (-0.5)
    query_grouped_four = queries.reshape(row_denominator_sum, kv_heads, groups, HD)
    key_four = key_rows.reshape(row_denominator_sum, context, kv_heads, HD)
    value_four = value_rows.reshape(row_denominator_sum, context, kv_heads, HD)
    current_key = new_keys.reshape(row_denominator_sum, kv_heads, HD)
    own_value = new_values.reshape(row_denominator_sum, kv_heads, HD).astype(jnp.float32)
    scores = (
        jnp.einsum(
            "bkgd,bckd->bkgc", query_grouped_four, key_four, preferred_element_type=jnp.float32
        )
        * attention_logit_scale
    )
    positions = jnp.arange(context, dtype=jnp.int32)
    valid_mask = positions[None, :] < context_len[:, None]
    scores = jnp.where(valid_mask[:, None, None, :], scores, masked_score)
    current_score = (
        jnp.einsum(
            "cnhz,cnz->cnh", query_grouped_four, current_key, preferred_element_type=jnp.float32
        )
        * attention_logit_scale
    )
    row_max = jnp.maximum(jnp.max(scores, axis=3), current_score)
    exponent = jnp.exp(scores - row_max[..., None])
    own_exponent = jnp.exp(current_score - row_max)
    denominator = jnp.sum(exponent, axis=3) + own_exponent
    weights = (exponent / denominator[..., None]).astype(jnp.bfloat16)
    own_weight = (own_exponent / denominator).astype(jnp.bfloat16).astype(jnp.float32)
    combined = jnp.einsum(
        "bkgc,bckd->bkgd", weights, value_four, preferred_element_type=jnp.float32
    )
    combined = combined + own_weight[..., None] * own_value[:, :, None, :]
    return combined.reshape(row_denominator_sum, -1).astype(jnp.bfloat16)


def body(
    queries,
    new_keys,
    new_values,
    key_cache,
    value_cache,
    context_len,
    cache_slot,
    residual_in,
    out_weight,
    gate_weight,
    up_weight,
):
    local_rows = queries.shape[0]
    row_base = lax.axis_index(("grp", "mr")) * local_rows
    device_slot_index = cache_slot - row_base
    positions = jnp.arange(local_rows, dtype=jnp.int32)
    matches = device_slot_index[:, None] == positions[None, :]
    inverse = jnp.sum(jnp.where(matches, positions[:, None], 0), axis=0)
    by_cache = attend_rows(
        jnp.take(queries, inverse, axis=0),
        jnp.take(new_keys, inverse, axis=0),
        jnp.take(new_values, inverse, axis=0),
        key_cache,
        value_cache,
        jnp.take(context_len, inverse, axis=0),
    )
    attended = jnp.take(by_cache, device_slot_index, axis=0)
    gathered = lax.all_gather(attended, "mc", axis=1, tiled=True)
    features = lax.all_to_all(gathered, ("grp", "mr"), split_axis=1, concat_axis=0, tiled=True)
    groups = lax.axis_size("grp")
    rows = features.shape[0]
    group_rows = rows // groups
    group = lax.axis_index("grp")
    own_share = None
    for shift in range(groups - 1, -1, -1):
        target = lax.rem(group + shift, groups)
        block = lax.dynamic_slice_in_dim(features, target * group_rows, group_rows, axis=0)
        term = jnp.dot(block, out_weight, preferred_element_type=jnp.float32)
        if shift > 0:
            pairs = [(i, (i + shift) % groups) for i in range(groups)]
            term = lax.ppermute(term.astype(jnp.bfloat16), "grp", pairs).astype(jnp.float32)
        own_share = term if own_share is None else own_share + term
    shares = lax.psum_scatter(
        own_share.astype(jnp.bfloat16), "mr", scatter_dimension=0, tiled=True
    ).astype(jnp.float32)
    residual_out = (residual_in.astype(jnp.float32) + shares).astype(jnp.bfloat16)
    group_part = lax.all_gather(residual_out, "mr", axis=0, tiled=True)
    everyone = lax.all_gather(group_part, "grp", axis=0, tiled=True) if groups != 2 else None
    if groups == 2:
        other_part = lax.ppermute(group_part, "grp", [(0, 1), (1, 0)])
        first = jnp.where(group == 0, group_part, other_part)
        second = jnp.where(group == 0, other_part, group_part)
        everyone = jnp.concatenate([first, second], axis=0)
    widened = lax.optimization_barrier(everyone).astype(jnp.float32)
    squares = jnp.sum(widened * widened, axis=1)
    square_sum = scatter_sum(squares, jnp.float32)
    gate_term = jnp.dot(everyone, gate_weight, preferred_element_type=jnp.float32)
    gate_sum = scatter_sum(gate_term, jnp.bfloat16)
    up_term = jnp.dot(everyone, up_weight, preferred_element_type=jnp.float32)
    up_sum = scatter_sum(up_term, jnp.bfloat16)
    inverse_rms = lax.rsqrt(square_sum / D + norm_epsilon)
    gate_value = gate_sum * inverse_rms[:, None]
    upward = up_sum * inverse_rms[:, None]
    activation = (jax.nn.silu(gate_value) * upward).astype(jnp.bfloat16)
    return (residual_out, activation)


def scatter_sum(term, kind):
    count = lax.axis_size("mc")
    me = lax.axis_index("mc")
    kept = term.shape[0] // count
    total = lax.dynamic_slice_in_dim(term, me * kept, kept, axis=0)
    for shift in range(1, count):
        target = lax.rem(me + shift, count)
        sent = lax.dynamic_slice_in_dim(term, target * kept, kept, axis=0).astype(kind)
        pairs = [(i, (i + shift) % count) for i in range(count)]
        total = total + lax.ppermute(sent, "mc", pairs).astype(jnp.float32)
    return total


def solution(mesh):
    in_specs = (
        P(("grp", "mr"), "mc"),
        P(("grp", "mr"), "mc"),
        P(("grp", "mr"), "mc"),
        P(("grp", "mr"), None, "mc"),
        P(("grp", "mr"), None, "mc"),
        P(("grp", "mr")),
        P(("grp", "mr")),
        P(("grp", "mr"), "mc"),
        P(("grp", "mr"), "mc"),
        P("mc", ("grp", "mr")),
        P("mc", ("grp", "mr")),
    )
    out_specs = (P(("grp", "mr"), "mc"), P("mc", ("grp", "mr")))
    return jax.shard_map(body, mesh=mesh, in_specs=in_specs, out_specs=out_specs, check_vma=False)
```
